128 devices in a mesh: seq: 4 (over z), exp: 32 (over y, x, core).
Axes of the slice: x: 4, y: 4, z: 4, core: 2. Of those that a mesh axis runs over, the one named last changes fastest.
Arguments:
- queries: bfloat16 [32, 256, 4096], P('exp', 'seq'), may hold values from -30 to 30
- key_heads: bfloat16 [32, 256, 512], P('exp', 'seq'), may hold values from -12 to 12
- value_heads: bfloat16 [32, 256, 512], P('exp', 'seq'), may hold values from -6 to 6
- residual: bfloat16 [32, 256, 4096], P('exp', 'seq'), may hold values from -16 to 16
- lengths: int32 [32, 6], P('exp'), may hold values from 1 to 128, 256 in all within a row
- routes: int32 [32, 256, 4], P('exp', 'seq'), may hold values from 0 to 31, all different within a row; in each aligned block of 64 rows (0 to 63, 64 to 127, ..., all dimensions but the last counted through in order) at most 10 rows name the same one
- gate_weights: bfloat16 [32, 256, 8], P('exp', 'seq'), may hold values from 0.049804688 to 0.29882812
- out_weight: bfloat16 [4096, 4096], P('seq', 'exp'), may hold values from -0.09375 to 0.09375
- norm_gain: float32 [4096], replicated, may hold values from 0.5 to 1.5
- w_gate: bfloat16 [32, 4, 4096, 768], P('exp', 'seq'), may hold values from -0.09375 to 0.09375
- w_up: bfloat16 [32, 4, 4096, 768], P('exp', 'seq'), may hold values from -0.09375 to 0.09375
- w_down: bfloat16 [32, 4, 768, 4096], P('exp', 'seq'), may hold values from -0.15625 to 0.15625
Outputs:
- result: bfloat16 [32, 256, 4096], P('exp', 'seq')
The draws below stay inside these ranges and needn't reach their ends.
Inputs may be any that keep to these rules, and one draw needn't show every extreme that they name: `lengths`: each row sums to 256, and its largest entry is 128. `routes`: the 4 entries of a token differ; among the rows of one device no column is named more than 10 times, a bound that some block reaches.
All inputs are finite; a program needn't handle non-finite values.
Results may differ from the reference program's by a relative error of at most 0.008.
Values may be sent and summed in bfloat16 or wider, within the bound.
No kernel may reach another device: no remote copies, remote signals or barrier semaphores. Data moves between devices by JAX's collectives and lax.ppermute only.
A program may use at most 128 MiB of HBM per device.

```python
import math
import jax
import jax.numpy as jnp
import numpy as np
from jax import lax

D = 4096
HQ = 32
KV_HEADS = 4
HEAD_DIM = 128
FF = 1536
EXP_COL = 2
NODES_TOK = 4
EPISODES = 6
TOK_DEV = 64
LENGTH = 256
PACKS = 32
MOST_LEN = 128
CAP = 10
TOP = 8
FF_PART = 768
N_SEQ = 4
N_EXP = 32


def draw_queries(key, part):
    noise_key = jax.random.fold_in(key, 11)
    drawn = jnp.clip(jax.random.normal(noise_key, (PACKS, LENGTH, HQ * HEAD_DIM), jnp.float32), -6.0, 6.0)
    return drawn.astype(jnp.bfloat16)


def draw_key_heads(key, part):
    noise_key = jax.random.fold_in(key, 12)
    drawn = jnp.clip(jax.random.normal(noise_key, (PACKS, LENGTH, KV_HEADS * HEAD_DIM), jnp.float32), -6.0, 6.0)
    return drawn.astype(jnp.bfloat16)


def draw_residual(key, part):
    noise_key = jax.random.fold_in(key, 21)
    drawn = jnp.clip(jax.random.normal(noise_key, (PACKS, LENGTH, D), jnp.float32), -6.0, 6.0)
    return drawn.astype(jnp.bfloat16)


def level_of(rng, dims, pieces, least, largest):
    gain = 1.0
    for dim, parts in pieces:
        heights = jax.random.uniform(jax.random.fold_in(jax.random.fold_in(rng, 6), dim), (parts,), jnp.float32, least / len(pieces), largest / len(pieces))
        gain = gain * jnp.repeat(jnp.exp(heights), dims[dim] // parts).reshape((-1,) + (1,) * (len(dims) - 1 - dim))
    return gain


def length_profile(count, total, reach, skew):
    weights = [(1 << 20) // math.isqrt(standing ** skew) + 1 for standing in range(2, count + 1)]
    surplus, holding = total - reach - (count - 1), [1] * (count - 1)
    while surplus > 0:
        movable = [i for i in range(count - 1) if holding[i] < reach]
        mass, left = sum([weights[i] for i in movable]), surplus
        for i in movable:
            addition = min(reach - holding[i], max(1, left * weights[i] // mass), surplus)
            holding[i] = holding[i] + addition
            surplus = surplus - addition
    return np.array([reach] + holding)


def ragged(own_key, amount, total, reach, skew):
    if amount == 2:
        one = jax.random.randint(own_key, (), max(1, total - reach), min(reach, total - 1) + 1)
        return jnp.stack([one, total - one])
    tallies = jnp.asarray(length_profile(amount, total, reach, skew), jnp.int32)
    twos = (amount - 1) // 2
    source_of, sink = tallies[1:1 + 2 * twos:2], tallies[2:2 + 2 * twos:2]
    room = jnp.minimum(source_of - 1, reach - sink)
    moved = jax.random.randint(jax.random.fold_in(own_key, 1), (twos,), 0, 1 << 20) % (room + 1)
    tallies = tallies.at[1:1 + 2 * twos:2].set(source_of - moved).at[2:2 + 2 * twos:2].set(sink + moved)
    return tallies[jax.random.permutation(jax.random.fold_in(own_key, 2), amount)]


def assign_block(rng, own, number, rows, amount, top, limit, skew):
    order = jax.random.permutation(rng, amount)
    packed, ordinary = shares(amount, rows * top, limit, skew, True), shares(amount, rows * top, limit, skew, False)
    places = jnp.arange(amount)

    def named(sizes, rotation):
        used = int((sizes > 0).sum())
        fixed = max(1, used // 4)
        passed = fixed + (places - fixed + rotation * (used - fixed)) % max(1, amount - fixed)
        return jnp.zeros((amount,), jnp.int32).at[order[jnp.where(places < fixed, places, passed)]].set(jnp.asarray(sizes, jnp.int32))

    sizes = jnp.where(number % 4 == 0, named(packed, number // 4), named(ordinary, number - number // 4 - 1))
    mixed = jax.random.permutation(jax.random.fold_in(own, 3), amount)
    source_of, taker = mixed[0:amount // 2 * 2:2], mixed[1:amount // 2 * 2:2]
    margin = jnp.minimum(sizes[source_of] - 1, limit - sizes[taker]) // 2
    margin = jnp.where((source_of == order[0]) | (taker == order[0]) | (sizes[taker] == 0), 0, jnp.maximum(margin, 0))
    passed = jax.random.randint(jax.random.fold_in(own, 4), (amount // 2,), 0, 1 << 20) % (margin + 1)
    sizes = sizes.at[source_of].add(-passed).at[taker].add(passed)
    members = jnp.searchsorted(jnp.cumsum(sizes), jnp.arange(rows * top), side="right").astype(jnp.int32)
    table = members.reshape(top, rows).T
    table = table[jax.random.permutation(jax.random.fold_in(own, 1), rows)]
    rotation = jax.random.randint(jax.random.fold_in(own, 2), (rows, 1), 0, top)
    return jnp.take_along_axis(table, (jnp.arange(top)[None, :] + rotation) % top, axis=1)


def shares(number_of, total, limit, skew, full):
    portions = [(1 << 20) // math.isqrt(rank ** skew) + 1 for rank in range(1, number_of + 1)]
    largest = limit if full else min(limit, max(-(-total // number_of), total * portions[0] // sum(portions)))
    least = 1 if total - largest >= number_of - 1 else 0
    counts, spare = [largest] + [least] * (number_of - 1), total - largest - least * (number_of - 1)
    while spare > 0:
        free = [i for i in range(1, number_of) if counts[i] < largest] or [i for i in range(1, number_of) if counts[i] < limit]
        whole, left = sum([portions[i] for i in free]), spare
        for i in free:
            addition = min(limit - counts[i], max(1, left * portions[i] // whole), spare)
            counts[i] = counts[i] + addition
            spare = spare - addition
    return np.array(counts)


def bell_draw(rng, extent, scale, limit, cuts=(), kind=jnp.bfloat16):
    drawn = jax.random.normal(rng, extent, jnp.float32) * scale
    if len(cuts) > 0:
        drawn = level_of(rng, extent, cuts, -0.22, 0.18) * drawn
    return jnp.clip(drawn, min=-limit, max=limit).astype(kind)


def setup_inputs(seed: int = 0) -> dict:
    seeds = jax.random.split(jax.random.key(seed), 13)
    queries = draw_queries(jax.random.fold_in(seeds[12], 71), 0)
    key_heads = draw_key_heads(jax.random.fold_in(seeds[12], 71), 0)
    value_heads = bell_draw(seeds[2], (PACKS, LENGTH, KV_HEADS * HEAD_DIM), 1.0, 6.0, ((0, 32), (1, 4)))
    residual = draw_residual(jax.random.fold_in(seeds[12], 71), 0)
    lengths = jax.vmap(lambda own: ragged(own, EPISODES, LENGTH, MOST_LEN, 2))(jax.random.split(seeds[4], PACKS)).reshape((PACKS, EPISODES)).astype(jnp.int32)
    routes_keys = jax.random.split(jax.random.fold_in(seeds[5], 1), PACKS * LENGTH // TOK_DEV)
    routes_turns = jax.random.permutation(jax.random.fold_in(seeds[5], 3), PACKS * LENGTH // TOK_DEV)
    routes = jax.vmap(lambda own, number: assign_block(jax.random.fold_in(seeds[5], 2), own, number, TOK_DEV, N_EXP, NODES_TOK, CAP, 2))(routes_keys, routes_turns).reshape((PACKS, LENGTH, NODES_TOK))
    gate_weights = jnp.clip(0.049804688 + 0.24902344 * jax.random.uniform(seeds[6], (PACKS, LENGTH, TOP), jnp.float32) ** level_of(seeds[6], (PACKS, LENGTH, TOP), ((0, 32), (1, 4)), -0.2, 0.2), 0.049804688, 0.29882812).astype(jnp.bfloat16)
    out_weight = bell_draw(seeds[7], (HQ * HEAD_DIM, D), (HQ * HEAD_DIM) ** -0.5, 0.09375, ((0, 4), (1, 32)))
    norm_gain = jnp.clip(1.0 + 0.1 * jax.random.normal(seeds[8], (D,), jnp.float32), 0.5, 1.5)
    w_gate = bell_draw(seeds[9], (N_EXP, N_SEQ, D, FF_PART), D ** -0.5, 0.09375, ((0, 32), (1, 4)))
    w_up = bell_draw(seeds[10], (N_EXP, N_SEQ, D, FF_PART), D ** -0.5, 0.09375, ((0, 32), (1, 4)))
    w_down = bell_draw(seeds[11], (N_EXP, N_SEQ, FF_PART, D), FF ** -0.5, 0.15625, ((0, 32), (1, 4)))
    return dict(queries=queries, key_heads=key_heads, value_heads=value_heads, residual=residual, lengths=lengths, routes=routes, gate_weights=gate_weights, out_weight=out_weight, norm_gain=norm_gain, w_gate=w_gate, w_up=w_up, w_down=w_down)


epsilon = 1e-06

def episode_ids(length_row, position_count):
    bounds = jnp.cumsum(length_row)
    position = jnp.arange(position_count, dtype=jnp.int32)
    return lax.optimization_barrier(jnp.sum((position[:, None] >= bounds[None, :]).astype(jnp.int32), axis=1))

def attend(query_rows, key_rows, value_rows, episode):
    row_count = query_rows.shape[0]
    groups = key_rows.shape[1] // HEAD_DIM
    per_group = query_rows.shape[1] // HEAD_DIM // groups
    q_heads = query_rows.astype(jnp.float32).reshape(row_count, groups, per_group, HEAD_DIM)
    k_heads = key_rows.astype(jnp.float32).reshape(row_count, groups, HEAD_DIM)
    v_heads = value_rows.astype(jnp.float32).reshape(row_count, groups, HEAD_DIM)
    scores = jnp.einsum('tgpd,ugd->gptu', q_heads, k_heads) / math.sqrt(HEAD_DIM)
    position = jnp.arange(row_count, dtype=jnp.int32)
    allowed = (episode[:, None] == episode[None, :]) & (position[None, :] <= position[:, None])
    scores = jnp.where(allowed, scores, -jnp.inf)
    row_maximum = lax.optimization_barrier(jnp.max(scores, axis=-1, keepdims=True))
    weights = jnp.exp(scores - row_maximum)
    probability = (weights / lax.optimization_barrier(jnp.sum(weights, axis=-1, keepdims=True))).astype(jnp.bfloat16)
    mixed = jnp.einsum('gptu,ugd->tgpd', probability.astype(jnp.float32), v_heads)
    return mixed.astype(jnp.bfloat16).reshape(row_count, groups * per_group * HEAD_DIM)

def reference(queries, key_heads, value_heads, residual, lengths, routes, gate_weights, out_weight, norm_gain, w_gate, w_up, w_down):

    def one_pack(pack_args):
        query_rows, key_rows, value_rows, length_row = pack_args
        return attend(query_rows, key_rows, value_rows, episode_ids(length_row, LENGTH))
    mixed = lax.map(one_pack, (queries, key_heads, value_heads, lengths))
    projected = jnp.dot(mixed.reshape(-1, HQ * HEAD_DIM), out_weight, preferred_element_type=jnp.float32)
    hidden = residual.reshape(-1, D).astype(jnp.float32) + projected
    inverse = lax.rsqrt(lax.optimization_barrier(jnp.mean(hidden * hidden, axis=1, keepdims=True)) + epsilon)
    normalized_rows = (hidden * inverse * norm_gain[None, :]).astype(jnp.bfloat16)
    routed = routes.reshape(-1, NODES_TOK)
    gate_pair = gate_weights.reshape(-1, NODES_TOK, EXP_COL).astype(jnp.float32)
    token_total = routed.shape[0]
    slot_limit = CAP * N_SEQ * N_EXP
    halves = N_SEQ // EXP_COL

    def column(carry_sum, column_id):
        on_node = routed == column_id
        member = jnp.any(on_node, axis=1)
        rank = jnp.cumsum(member.astype(jnp.int32)) - 1
        slot = jnp.where(member, rank, slot_limit)
        row_index = jnp.zeros((slot_limit + 1,), jnp.int32).at[slot].set(jnp.arange(token_total, dtype=jnp.int32))[:slot_limit]
        valid_slot = jnp.zeros((slot_limit + 1,), jnp.float32).at[slot].set(1.0)[:slot_limit]
        token_rows = normalized_rows[row_index]
        node_route_gate = lax.optimization_barrier(jnp.sum(jnp.where(on_node[:, :, None], gate_pair, 0.0), axis=1))[row_index]
        gate_block = w_gate[column_id]
        up_block = w_up[column_id]
        down_block = w_down[column_id]
        accum_sum = jnp.zeros((slot_limit, D), jnp.float32)
        for expert_slot in range(EXP_COL):
            for half_slot in range(halves):
                entry = expert_slot * halves + half_slot
                gate_proj = jnp.dot(token_rows, gate_block[entry], preferred_element_type=jnp.float32)
                up_proj = jnp.dot(token_rows, up_block[entry], preferred_element_type=jnp.float32)
                activated = (jax.nn.silu(gate_proj) * up_proj).astype(jnp.bfloat16)
                partial_value = jnp.dot(activated, down_block[entry], preferred_element_type=jnp.float32).astype(jnp.bfloat16)
                partial_value = lax.optimization_barrier(partial_value)
                weighted = (partial_value.astype(jnp.float32) * node_route_gate[:, expert_slot:expert_slot + 1]).astype(jnp.bfloat16)
                weighted = lax.optimization_barrier(weighted)
                accum_sum = accum_sum + weighted.astype(jnp.float32)
        node_sum = lax.optimization_barrier(accum_sum.astype(jnp.bfloat16))
        node_sum = node_sum.astype(jnp.float32) * valid_slot[:, None]
        return (carry_sum.at[row_index].add(node_sum), None)
    mixture_expert_total, _ = lax.scan(column, jnp.zeros((token_total, D), jnp.float32), jnp.arange(N_EXP, dtype=jnp.int32))
    return (hidden + mixture_expert_total).astype(jnp.bfloat16).reshape(PACKS, LENGTH, D)
```

```python
import math

import jax
import jax.numpy as jnp
from jax import lax
from jax.sharding import PartitionSpec as P

HEAD_DIM = 128
EXP_COL = 2


epsilon = 1e-06


def episode_ids(length_row, position_count):
    bounds = jnp.cumsum(length_row)
    position = jnp.arange(position_count, dtype=jnp.int32)
    return jnp.sum((position[:, None] >= bounds[None, :]).astype(jnp.int32), axis=1)


def attend(query_rows, key_rows, value_rows, episode):
    row_count = query_rows.shape[0]
    groups = key_rows.shape[1] // HEAD_DIM
    per_group = query_rows.shape[1] // HEAD_DIM // groups
    q_heads = query_rows.reshape(row_count, groups, per_group, HEAD_DIM)
    k_heads = key_rows.reshape(row_count, groups, HEAD_DIM)
    v_heads = value_rows.reshape(row_count, groups, HEAD_DIM)
    scores = jnp.einsum(
        "tgpd,ugd->gptu", q_heads, k_heads, preferred_element_type=jnp.float32
    ) / math.sqrt(HEAD_DIM)
    position = jnp.arange(row_count, dtype=jnp.int32)
    allowed = (episode[:, None] == episode[None, :]) & (position[None, :] <= position[:, None])
    scores = jnp.where(allowed, scores, -jnp.inf)
    row_maximum = jnp.max(scores, axis=-1, keepdims=True)
    weights = jnp.exp(scores - row_maximum)
    probability = (weights / jnp.sum(weights, axis=-1, keepdims=True)).astype(jnp.bfloat16)
    mixed = jnp.einsum("gptu,ugd->tgpd", probability, v_heads, preferred_element_type=jnp.float32)
    return mixed.astype(jnp.bfloat16).reshape(row_count, groups * per_group * HEAD_DIM)


CHUNKS = (2, 4, 4)


def ring(rows, step):
    count = lax.axis_size("seq")
    return lax.ppermute(rows, "seq", [(i, (i + step) % count) for i in range(count)])


def add(*parts):
    return sum(p.astype(jnp.float32) for p in parts).astype(jnp.bfloat16)


def gather_ring(rows):
    half = rows.shape[0] // 2
    left, right = ring(rows, 1), ring(rows, -1)
    far_a, far_b = ring(left[:half], 1), ring(right[half:], -1)
    return [rows, left, right, far_a, far_b]


def scatter_ring(own, left, right, far):
    half = own.shape[0] // 2
    far_a, far_b = ring(far[:half], 1), ring(far[half:], -1)
    from_left_b, from_right_a = ring(right[half:], 1), ring(left[:half], -1)
    from_left_a = ring(add(right[:half], far_a), 1)
    from_right_b = ring(add(left[half:], far_b), -1)
    return jnp.concatenate(
        [
            add(own[:half], from_left_a, from_right_a),
            add(own[half:], from_left_b, from_right_b),
        ],
        axis=0,
    )


def across(blocks):
    return lax.all_to_all(blocks, "exp", split_axis=0, concat_axis=0, tiled=True)


def local(
    queries,
    key_heads,
    value_heads,
    residual,
    lengths,
    routes,
    gate_weights,
    out_weight,
    norm_gain,
    w_gate,
    w_up,
    w_down,
):
    columns = lax.axis_size("exp")
    token_count = residual.shape[1]
    model_width = residual.shape[2]

    routed = routes[0]
    node_count = routed.shape[1]
    capacity = max(2, 5 * token_count * node_count // (4 * columns))
    on_node = routed[:, :, None] == jnp.arange(columns, dtype=jnp.int32)[None, None, :]
    member = jnp.sum(on_node.astype(jnp.int32), axis=1)
    before = jnp.cumsum(member, axis=0) - member
    slot_lookup_index = (
        before[:, :, None] == jnp.arange(capacity, dtype=jnp.int32)[None, None, :]
    ) & (member[:, :, None] > 0)
    slot_flag_mask = slot_lookup_index.astype(jnp.bfloat16)
    gate_pair = gate_weights[0].reshape(token_count, node_count, EXP_COL).astype(jnp.float32)
    node_route_gate = jnp.einsum(
        "tnc,tne->tce", on_node.astype(jnp.float32), gate_pair, precision=lax.Precision.HIGHEST
    )
    slot_gate = jnp.einsum(
        "qnr,qny->nyr",
        slot_lookup_index.astype(jnp.float32),
        node_route_gate,
        precision=lax.Precision.HIGHEST,
    ).astype(jnp.bfloat16)
    gate_in = across(slot_gate.reshape(columns, EXP_COL * capacity))
    expert_pick = lax.axis_index("seq") // (lax.axis_size("seq") // EXP_COL)
    gates = [
        lax.dynamic_index_in_dim(
            g.reshape(columns, EXP_COL, capacity), expert_pick, axis=1, keepdims=False
        ).astype(jnp.float32)
        for g in (gate_in, ring(gate_in, 1), ring(gate_in, -1), ring(gate_in, 2))
    ]

    whole_q, whole_k, whole_v = (
        lax.all_to_all(queries[0], "seq", split_axis=1, concat_axis=0, tiled=True),
        lax.all_to_all(key_heads[0], "seq", split_axis=1, concat_axis=0, tiled=True),
        lax.all_to_all(value_heads[0], "seq", split_axis=1, concat_axis=0, tiled=True),
    )
    episode = episode_ids(lengths[0], whole_q.shape[0])
    mixed = attend(whole_q, whole_k, whole_v, episode)
    head_partial = jnp.dot(
        mixed,
        lax.all_gather(out_weight, "exp", axis=1, tiled=True),
        preferred_element_type=jnp.float32,
    )
    projected = lax.psum_scatter(
        head_partial.astype(jnp.bfloat16), "seq", scatter_dimension=0, tiled=True
    ).astype(jnp.float32)
    hidden = residual[0].astype(jnp.float32) + projected
    inverse = lax.rsqrt(jnp.mean(hidden * hidden, axis=1, keepdims=True) + epsilon)
    normalized_rows = (hidden * inverse * norm_gain[None, :]).astype(jnp.bfloat16)

    gate_block, up_block, down_block = w_gate[0, 0], w_up[0, 0], w_down[0, 0]
    total = hidden
    at = 0
    for size in CHUNKS:
        flags = slot_flag_mask[:, :, at : at + size]
        outbound = jnp.einsum(
            "roj,rm->ojm", flags, normalized_rows, preferred_element_type=jnp.float32
        ).astype(jnp.bfloat16)
        rows_in = across(outbound).reshape(columns * size, model_width)
        rows = jnp.concatenate(gather_ring(rows_in), axis=0)
        gate = jnp.concatenate([g[:, at : at + size].reshape(-1) for g in gates])
        gate_proj = jnp.dot(rows, gate_block, preferred_element_type=jnp.float32)
        up_proj = jnp.dot(rows, up_block, preferred_element_type=jnp.float32)
        activated = (jax.nn.silu(gate_proj) * up_proj).astype(jnp.bfloat16)
        partial_value = jnp.dot(activated, down_block, preferred_element_type=jnp.float32)
        gated = (
            partial_value.astype(jnp.bfloat16).astype(jnp.float32) * gate[:, None]
        ).astype(jnp.bfloat16)
        block = columns * size
        node_sum = scatter_ring(*(gated[i * block : (i + 1) * block] for i in range(4)))
        back = across(node_sum.reshape(columns, size, model_width))
        total = total + jnp.einsum("gyr,yre->ge", flags, back, preferred_element_type=jnp.float32)
        at += size
    return total.astype(jnp.bfloat16)[None]


def solution(mesh):
    return jax.shard_map(
        local,
        mesh=mesh,
        in_specs=(
            P("exp", "seq", None),
            P("exp", "seq", None),
            P("exp", "seq", None),
            P("exp", "seq", None),
            P("exp", None),
            P("exp", "seq", None),
            P("exp", "seq", None),
            P("seq", "exp"),
            P(),
            P("exp", "seq", None, None),
            P("exp", "seq", None, None),
            P("exp", "seq", None, None),
        ),
        out_specs=P("exp", "seq", None),
        check_vma=False,
    )
```

```python
import functools
import math

import jax
import jax.numpy as jnp
from jax import lax
from jax.experimental import pallas as pl
from jax.experimental.pallas import tpu as pltpu
from jax.sharding import PartitionSpec as P

HEAD_DIM = 128
EXP_COL = 2


epsilon = 1e-06


def episode_ids(length_row, position_count):
    bounds = jnp.cumsum(length_row)
    position = jnp.arange(position_count, dtype=jnp.int32)
    return jnp.sum((position[:, None] >= bounds[None, :]).astype(jnp.int32), axis=1)


def attend(query_rows, key_rows, value_rows, episode):
    row_count = query_rows.shape[0]
    groups = key_rows.shape[1] // HEAD_DIM
    per_group = query_rows.shape[1] // HEAD_DIM // groups
    q_heads = query_rows.reshape(row_count, groups, per_group, HEAD_DIM)
    k_heads = key_rows.reshape(row_count, groups, HEAD_DIM)
    v_heads = value_rows.reshape(row_count, groups, HEAD_DIM)
    scores = jnp.einsum(
        "tgpd,ugd->gptu", q_heads, k_heads, preferred_element_type=jnp.float32
    ) / math.sqrt(HEAD_DIM)
    position = jnp.arange(row_count, dtype=jnp.int32)
    allowed = (episode[:, None] == episode[None, :]) & (position[None, :] <= position[:, None])
    scores = jnp.where(allowed, scores, -jnp.inf)
    row_maximum = jnp.max(scores, axis=-1, keepdims=True)
    weights = jnp.exp(scores - row_maximum)
    probability = (weights / jnp.sum(weights, axis=-1, keepdims=True)).astype(jnp.bfloat16)
    mixed = jnp.einsum("gptu,ugd->tgpd", probability, v_heads, preferred_element_type=jnp.float32)
    return mixed.astype(jnp.bfloat16).reshape(row_count, groups * per_group * HEAD_DIM)


SHARED_SLOTS = 6
TILE_ROWS = 8


HIDDEN_BLOCK = 256
OUT_BLOCK = 1024


def expert_kernel(hidden_steps, rows_ref, gate_ref, wg_ref, wu_ref, wd_ref, out_ref, act_ref):
    step = pl.program_id(0)

    @pl.when(step < hidden_steps)
    def _():
        x = rows_ref[...]
        g = jnp.dot(x, wg_ref[...], preferred_element_type=jnp.float32)
        u = jnp.dot(x, wu_ref[...], preferred_element_type=jnp.float32)
        act_ref[step] = (g / (1.0 + jnp.exp(-g)) * u).astype(jnp.bfloat16)

    @pl.when(step >= hidden_steps)
    def _():
        y = sum(
            jnp.dot(
                act_ref[b],
                wd_ref[pl.ds(b * HIDDEN_BLOCK, HIDDEN_BLOCK)],
                preferred_element_type=jnp.float32,
            )
            for b in range(hidden_steps)
        )
        y = y.astype(jnp.bfloat16).astype(jnp.float32) * gate_ref[...]
        out_ref[...] = y.astype(jnp.bfloat16)


def expert(rows, gate, w_gate, w_up, w_down):
    width, ff = w_gate.shape
    total = rows.shape[0]
    hidden_steps, out_steps = ff // HIDDEN_BLOCK, width // OUT_BLOCK

    def hidden_map(i):
        return (0, jnp.minimum(i, hidden_steps - 1))

    def out_map(i):
        return (0, jnp.maximum(i - hidden_steps, 0))

    return pl.pallas_call(
        functools.partial(expert_kernel, hidden_steps),
        grid=(hidden_steps + out_steps,),
        in_specs=[
            pl.BlockSpec((total, width), lambda i: (0, 0), pipeline_mode=pl.Buffered(1)),
            pl.BlockSpec((total, 1), lambda i: (0, 0), pipeline_mode=pl.Buffered(1)),
            pl.BlockSpec((width, HIDDEN_BLOCK), hidden_map),
            pl.BlockSpec((width, HIDDEN_BLOCK), hidden_map),
            pl.BlockSpec((ff, OUT_BLOCK), out_map),
        ],
        out_specs=pl.BlockSpec((total, OUT_BLOCK), out_map),
        out_shape=jax.ShapeDtypeStruct((total, width), jnp.bfloat16),
        scratch_shapes=[pltpu.VMEM((hidden_steps, total, HIDDEN_BLOCK), jnp.bfloat16)],
        compiler_params=pltpu.CompilerParams(vmem_limit_bytes=50 * 1024 * 1024),
        cost_estimate=pl.CostEstimate(
            flops=6 * total * width * ff,
            transcendentals=total * ff,
            bytes_accessed=2 * (3 * width * ff + 2 * total * width),
        ),
        name="expert",
    )(rows, gate, w_gate, w_up, w_down)


def ring(rows, step):
    count = lax.axis_size("seq")
    return lax.ppermute(rows, "seq", [(i, (i + step) % count) for i in range(count)])


def around(rows):
    return [rows] + [ring(rows, -k) for k in range(1, lax.axis_size("seq"))]


def in_order(parts):
    count = len(parts)
    start = lax.rem(count - lax.axis_index("seq"), count)
    return lax.dynamic_slice_in_dim(jnp.stack(parts + parts), start, count, axis=0)


def across(blocks):
    return lax.all_to_all(blocks, "exp", split_axis=0, concat_axis=0, tiled=True)


def across_slots(blocks):
    columns, slots, width = blocks.shape
    flat = blocks.reshape(columns, slots * TILE_ROWS, width // TILE_ROWS)
    return across(flat).reshape(columns, slots, width)


def local(
    queries,
    key_heads,
    value_heads,
    residual,
    lengths,
    routes,
    gate_weights,
    out_weight,
    norm_gain,
    w_gate,
    w_up,
    w_down,
):
    columns = lax.axis_size("exp")
    token_count = residual.shape[1]
    model_width = residual.shape[2]

    routed = routes[0]
    node_count = routed.shape[1]
    capacity = max(2, 5 * token_count * node_count // (4 * columns))
    column = jnp.arange(columns, dtype=jnp.int32)
    slot = jnp.arange(capacity, dtype=jnp.int32)

    def slots_of(named):
        on_node = named[:, :, None] == column[None, None, :]
        member = jnp.sum(on_node.astype(jnp.int32), axis=1)
        before = jnp.cumsum(member, axis=0) - member
        return on_node, (before[:, :, None] == slot[None, None, :]) & (member[:, :, None] > 0)

    on_node, lookup = slots_of(routed)
    lookups = [slots_of(named)[1] for named in around(routed)]
    gate_pair = gate_weights[0].reshape(token_count, node_count, EXP_COL).astype(jnp.float32)
    node_route_gate = jnp.einsum(
        "tnc,tne->tce", on_node.astype(jnp.float32), gate_pair, precision=lax.Precision.HIGHEST
    )
    slot_gate = jnp.einsum(
        "qnr,qny->nyr",
        lookup.astype(jnp.float32),
        node_route_gate,
        precision=lax.Precision.HIGHEST,
    ).astype(jnp.bfloat16)
    gate_in = across(slot_gate.reshape(columns, EXP_COL * capacity))
    expert_pick = lax.axis_index("seq") // (lax.axis_size("seq") // EXP_COL)
    gates = [
        lax.dynamic_index_in_dim(
            g.reshape(columns, EXP_COL, capacity), expert_pick, axis=1, keepdims=False
        ).astype(jnp.float32)
        for g in around(gate_in)
    ]
    direct = capacity - SHARED_SLOTS
    shared_mask = lookup[:, :, :SHARED_SLOTS].astype(jnp.bfloat16)
    shared_gate = in_order([g[:, :SHARED_SLOTS].reshape(-1) for g in gates]).reshape(-1, 1)
    direct_gate = jnp.stack([g[:, SHARED_SLOTS:] for g in gates], axis=1).reshape(-1, 1)
    offset = jnp.arange(len(lookups))
    direct_masks = [
        (m[:, :, None, SHARED_SLOTS:] & (offset[None, None, :, None] == i))
        .reshape(token_count, -1)
        .astype(jnp.bfloat16)
        for i, m in enumerate(lookups)
    ]
    send_mask = jnp.concatenate(direct_masks, axis=0)
    sum_mask = in_order(direct_masks).reshape(send_mask.shape)

    whole_q, whole_k, whole_v = (
        lax.all_to_all(queries[0], "seq", split_axis=1, concat_axis=0, tiled=True),
        lax.all_to_all(key_heads[0], "seq", split_axis=1, concat_axis=0, tiled=True),
        lax.all_to_all(value_heads[0], "seq", split_axis=1, concat_axis=0, tiled=True),
    )
    episode = episode_ids(lengths[0], whole_q.shape[0])
    mixed = attend(whole_q, whole_k, whole_v, episode)
    mixed, shared_gate, direct_gate, send_mask, sum_mask = lax.optimization_barrier(
        (mixed, shared_gate, direct_gate, send_mask, sum_mask)
    )
    head_partial = jnp.dot(
        mixed,
        lax.all_gather(out_weight, "exp", axis=1, tiled=True),
        preferred_element_type=jnp.float32,
    )
    projected = lax.psum_scatter(
        head_partial.astype(jnp.bfloat16), "seq", scatter_dimension=0, tiled=True
    ).astype(jnp.float32)
    hidden = residual[0].astype(jnp.float32) + projected
    inverse = lax.rsqrt(jnp.mean(hidden * hidden, axis=1, keepdims=True) + epsilon)
    normalized_rows = (hidden * inverse * norm_gain[None, :]).astype(jnp.bfloat16)

    gate_block, up_block, down_block = w_gate[0, 0], w_up[0, 0], w_down[0, 0]
    weights = (gate_block, up_block, down_block)
    shared_out = jnp.einsum(
        "roj,rm->ojm", shared_mask, normalized_rows, preferred_element_type=jnp.float32
    ).astype(jnp.bfloat16)
    shared_in, pack_rows = lax.optimization_barrier(
        (across_slots(shared_out).reshape(-1, model_width), around(normalized_rows))
    )
    shared_rows = lax.all_gather(shared_in, "seq", axis=0, tiled=True)
    direct_out = jnp.einsum(
        "rq,rm->qm",
        send_mask,
        jnp.concatenate(pack_rows, axis=0),
        preferred_element_type=jnp.float32,
    ).astype(jnp.bfloat16)
    direct_count = direct_out.shape[0]
    direct_rows = across(direct_out.reshape(columns, -1, model_width))
    shared_rows, direct_rows = lax.optimization_barrier((shared_rows, direct_rows))
    shared_parts = expert(shared_rows, shared_gate, *weights)
    direct_parts = expert(direct_rows.reshape(direct_count, model_width), direct_gate, *weights)
    direct_back = across(direct_parts.reshape(columns, -1, model_width))
    shared_sums = lax.psum_scatter(shared_parts, "seq", scatter_dimension=0, tiled=True)
    shared_sums, direct_back = lax.optimization_barrier((shared_sums, direct_back))
    shared_back = across_slots(shared_sums.reshape(columns, SHARED_SLOTS, model_width))
    pack_sums = jnp.einsum(
        "rq,qm->rm",
        sum_mask,
        direct_back.reshape(direct_count, model_width),
        preferred_element_type=jnp.float32,
    ).astype(jnp.bfloat16)
    direct_sums = lax.psum_scatter(pack_sums, "seq", scatter_dimension=0, tiled=True)
    total = hidden + jnp.einsum(
        "gyr,yre->ge", shared_mask, shared_back, preferred_element_type=jnp.float32
    )
    total = total + direct_sums.astype(jnp.float32)
    return total.astype(jnp.bfloat16)[None]


def solution(mesh):
    return jax.shard_map(
        local,
        mesh=mesh,
        in_specs=(
            P("exp", "seq", None),
            P("exp", "seq", None),
            P("exp", "seq", None),
            P("exp", "seq", None),
            P("exp", None),
            P("exp", "seq", None),
            P("exp", "seq", None),
            P("seq", "exp"),
            P(),
            P("exp", "seq", None, None),
            P("exp", "seq", None, None),
            P("exp", "seq", None, None),
        ),
        out_specs=P("exp", "seq", None),
        check_vma=False,
    )
```

```python
import functools
import math

import jax
import jax.numpy as jnp
from jax import lax
from jax.experimental import pallas as pl
from jax.experimental.pallas import tpu as pltpu
from jax.sharding import PartitionSpec as P

HEAD_DIM = 128
EXP_COL = 2


epsilon = 1e-06


def episode_ids(length_row, position_count):
    bounds = jnp.cumsum(length_row)
    position = jnp.arange(position_count, dtype=jnp.int32)
    return jnp.sum((position[:, None] >= bounds[None, :]).astype(jnp.int32), axis=1)


def attend(query_rows, key_rows, value_rows, episode):
    row_count = query_rows.shape[0]
    groups = key_rows.shape[1] // HEAD_DIM
    per_group = query_rows.shape[1] // HEAD_DIM // groups
    q_heads = query_rows.reshape(row_count, groups, per_group, HEAD_DIM)
    k_heads = key_rows.reshape(row_count, groups, HEAD_DIM)
    v_heads = value_rows.reshape(row_count, groups, HEAD_DIM)
    scores = jnp.einsum(
        "tgpd,ugd->gptu", q_heads, k_heads, preferred_element_type=jnp.float32
    ) / math.sqrt(HEAD_DIM)
    position = jnp.arange(row_count, dtype=jnp.int32)
    allowed = (episode[:, None] == episode[None, :]) & (position[None, :] <= position[:, None])
    scores = jnp.where(allowed, scores, -jnp.inf)
    row_maximum = jnp.max(scores, axis=-1, keepdims=True)
    weights = jnp.exp(scores - row_maximum)
    probability = (weights / jnp.sum(weights, axis=-1, keepdims=True)).astype(jnp.bfloat16)
    mixed = jnp.einsum("gptu,ugd->tgpd", probability, v_heads, preferred_element_type=jnp.float32)
    return mixed.astype(jnp.bfloat16).reshape(row_count, groups * per_group * HEAD_DIM)


SHARED_SLOTS = 6
TILE_ROWS = 8


CHUNK = 1024


def expert_kernel(sizes, places, aliased, *refs):
    count = len(sizes)
    pieces, (gate_ref, wg_ref, wu_ref, wd_ref) = refs[:count], refs[count : count + 4]
    out_ref, x_ref, wg_buf, wu_buf, wd_buf, g_ref, u_ref, y_ref, in_sems, out_sems = refs[
        count + 4 + aliased :
    ]
    chunks, out_chunks = x_ref.shape[0], wd_buf.shape[0]
    seats = out_ref.shape[0]
    seat = lax.axis_index("seq") if seats > 1 else 0

    def span(at):
        return pl.ds(pl.multiple_of(at * CHUNK, CHUNK), CHUNK)

    def loads(k):
        at = 0
        for i, size in enumerate(sizes):
            yield pltpu.make_async_copy(
                pieces[i].at[:, span(k)], x_ref.at[k, pl.ds(at, size)], in_sems.at[k, i]
            )
            at += size
        yield pltpu.make_async_copy(wg_ref.at[span(k)], wg_buf.at[k], in_sems.at[k, count])
        yield pltpu.make_async_copy(wu_ref.at[span(k)], wu_buf.at[k], in_sems.at[k, count + 1])

    def down_load(n):
        return pltpu.make_async_copy(
            wd_ref.at[:, span(n)], wd_buf.at[n], in_sems.at[n, count + 2]
        )

    def stores(n):
        slot = lax.rem(n, 2)
        for i, (offset, start, size) in enumerate(places):
            yield pltpu.make_async_copy(
                y_ref.at[slot, pl.ds(start, size)],
                out_ref.at[lax.rem(seat + offset, seats), :, span(n)],
                out_sems.at[slot, i],
            )

    for k in range(chunks):
        for c in loads(k):
            c.start()
    for n in range(out_chunks):
        down_load(n).start()

    g_ref[...] = jnp.zeros_like(g_ref)
    u_ref[...] = jnp.zeros_like(u_ref)

    def up(k, carry):
        for c in loads(k):
            c.wait()
        x = x_ref[k]
        g_ref[...] += jnp.dot(x, wg_buf[k], preferred_element_type=jnp.float32)
        u_ref[...] += jnp.dot(x, wu_buf[k], preferred_element_type=jnp.float32)
        return carry

    lax.fori_loop(0, chunks, up, 0)
    g = g_ref[...]
    act = (g / (1.0 + jnp.exp(-g)) * u_ref[...]).astype(jnp.bfloat16)

    def down(n, carry):
        down_load(n).wait()

        @pl.when(n >= 2)
        def _():
            for c in stores(n - 2):
                c.wait()

        y = jnp.dot(act, wd_buf[n], preferred_element_type=jnp.float32)
        y = y.astype(jnp.bfloat16).astype(jnp.float32) * gate_ref[...]
        y_ref[lax.rem(n, 2)] = y.astype(jnp.bfloat16)
        for c in stores(n):
            c.start()
        return carry

    lax.fori_loop(0, out_chunks, down, 0)
    for n in (out_chunks - 2, out_chunks - 1):
        for c in stores(n):
            c.wait()


def expert(pieces, gate, w_gate, w_up, w_down, seats, places, into=None):
    width, ff = w_gate.shape
    sizes = tuple(p.shape[0] for p in pieces)
    total = sum(sizes)
    chunks = width // CHUNK
    any_space = pl.BlockSpec(memory_space=pl.ANY)
    aliased = 0 if into is None else 1
    return pl.pallas_call(
        functools.partial(expert_kernel, sizes, places, aliased),
        in_specs=[any_space for _ in pieces]
        + [pl.BlockSpec(memory_space=pltpu.VMEM)]
        + [any_space] * (3 + aliased),
        out_specs=any_space,
        out_shape=jax.ShapeDtypeStruct((seats, places[0][2], width), jnp.bfloat16),
        scratch_shapes=[
            pltpu.VMEM((chunks, total, CHUNK), jnp.bfloat16),
            pltpu.VMEM((chunks, CHUNK, ff), jnp.bfloat16),
            pltpu.VMEM((chunks, CHUNK, ff), jnp.bfloat16),
            pltpu.VMEM((chunks, ff, CHUNK), jnp.bfloat16),
            pltpu.VMEM((total, ff), jnp.float32),
            pltpu.VMEM((total, ff), jnp.float32),
            pltpu.VMEM((2, total, CHUNK), jnp.bfloat16),
            pltpu.SemaphoreType.DMA((chunks, len(pieces) + 3)),
            pltpu.SemaphoreType.DMA((2, len(places))),
        ],
        input_output_aliases={len(pieces) + 4: 0} if aliased else {},
        compiler_params=pltpu.CompilerParams(vmem_limit_bytes=50 * 1024 * 1024),
        cost_estimate=pl.CostEstimate(
            flops=6 * total * width * ff,
            transcendentals=total * ff,
            bytes_accessed=2 * (3 * width * ff + 2 * total * width),
        ),
        name="expert",
    )(*pieces, gate, w_gate, w_up, w_down, *(() if into is None else (into,)))


def ring(rows, step):
    count = lax.axis_size("seq")
    return lax.ppermute(rows, "seq", [(i, (i + step) % count) for i in range(count)])


def around(rows):
    return [rows] + [ring(rows, -k) for k in range(1, lax.axis_size("seq"))]


def back_around(parts):
    return [parts[0]] + [ring(p, k) for k, p in enumerate(parts) if k]


def gather_ring(rows):
    half = rows.shape[0] // 2
    left, right = ring(rows, 1), ring(rows, -1)
    return [rows, right, left], [ring(left[:half], 1), ring(right[half:], -1)]


def across(blocks):
    return lax.all_to_all(blocks, "exp", split_axis=0, concat_axis=0, tiled=True)


def local(
    queries,
    key_heads,
    value_heads,
    residual,
    lengths,
    routes,
    gate_weights,
    out_weight,
    norm_gain,
    w_gate,
    w_up,
    w_down,
):
    columns = lax.axis_size("exp")
    token_count = residual.shape[1]
    model_width = residual.shape[2]

    routed = routes[0]
    node_count = routed.shape[1]
    capacity = max(2, 5 * token_count * node_count // (4 * columns))
    column = jnp.arange(columns, dtype=jnp.int32)
    slot = jnp.arange(capacity, dtype=jnp.int32)

    def slots_of(named):
        on_node = named[:, :, None] == column[None, None, :]
        member = jnp.sum(on_node.astype(jnp.int32), axis=1)
        before = jnp.cumsum(member, axis=0) - member
        return on_node, (before[:, :, None] == slot[None, None, :]) & (member[:, :, None] > 0)

    on_node, lookup = slots_of(routed)
    lookups = [slots_of(named)[1] for named in around(routed)]
    gate_pair = gate_weights[0].reshape(token_count, node_count, EXP_COL).astype(jnp.float32)
    node_route_gate = jnp.einsum(
        "tnc,tne->tce", on_node.astype(jnp.float32), gate_pair, precision=lax.Precision.HIGHEST
    )
    slot_gate = jnp.einsum(
        "qnr,qny->nyr",
        lookup.astype(jnp.float32),
        node_route_gate,
        precision=lax.Precision.HIGHEST,
    ).astype(jnp.bfloat16)
    gate_in = across(slot_gate.reshape(columns, EXP_COL * capacity))
    expert_pick = lax.axis_index("seq") // (lax.axis_size("seq") // EXP_COL)
    gates = [
        lax.dynamic_index_in_dim(
            g.reshape(columns, EXP_COL, capacity), expert_pick, axis=1, keepdims=False
        ).astype(jnp.float32)
        for g in around(gate_in)
    ]
    direct = capacity - SHARED_SLOTS
    part = jnp.arange(TILE_ROWS)
    shared_mask = (
        (
            lookup[:, :, :SHARED_SLOTS].transpose(1, 2, 0)[:, :, None, None, :]
            & (part[:, None] == part[None, :])[None, None, :, :, None]
        )
        .reshape(columns * SHARED_SLOTS * TILE_ROWS, TILE_ROWS * token_count)
        .astype(jnp.bfloat16)
    )
    ring_gates = [g[:, :SHARED_SLOTS].reshape(-1) for g in gates]
    near_gate = jnp.concatenate([ring_gates[i] for i in (0, 1, 3)])[:, None]
    far_gate = ring_gates[2][:, None]
    direct_gate = jnp.stack([g[:, SHARED_SLOTS:] for g in gates], axis=1).reshape(-1, 1)
    offset = jnp.arange(len(lookups))
    direct_masks = [
        (m[:, :, None, SHARED_SLOTS:] & (offset[None, None, :, None] == i))
        .reshape(token_count, -1)
        .astype(jnp.bfloat16)
        for i, m in enumerate(lookups)
    ]
    direct_mask = jnp.concatenate(direct_masks, axis=0)

    whole_q, whole_k, whole_v = (
        lax.all_to_all(queries[0], "seq", split_axis=1, concat_axis=0, tiled=True),
        lax.all_to_all(key_heads[0], "seq", split_axis=1, concat_axis=0, tiled=True),
        lax.all_to_all(value_heads[0], "seq", split_axis=1, concat_axis=0, tiled=True),
    )
    episode = episode_ids(lengths[0], whole_q.shape[0])
    mixed = attend(whole_q, whole_k, whole_v, episode)
    mixed, near_gate, far_gate, direct_gate, direct_mask, shared_mask = (
        lax.optimization_barrier(
            (mixed, near_gate, far_gate, direct_gate, direct_mask, shared_mask)
        )
    )
    turned = lax.dynamic_slice_in_dim(
        jnp.concatenate([mixed, mixed], axis=0),
        lax.axis_index("seq") * token_count,
        mixed.shape[0],
        axis=0,
    )
    head_partial = jnp.dot(
        turned,
        lax.all_gather(out_weight, "exp", axis=1, tiled=True),
        preferred_element_type=jnp.float32,
    ).astype(jnp.bfloat16)

    def by_owner(rows):
        return [rows[i : i + token_count] for i in range(0, rows.shape[0], token_count)]

    hidden = residual[0].astype(jnp.float32)
    for part in back_around(by_owner(head_partial)):
        hidden = hidden + part.astype(jnp.float32)
    inverse = lax.rsqrt(jnp.mean(hidden * hidden, axis=1, keepdims=True) + epsilon)
    normalized_rows = (hidden * inverse * norm_gain[None, :]).astype(jnp.bfloat16)

    gate_block, up_block, down_block = w_gate[0, 0], w_up[0, 0], w_down[0, 0]
    weights = (gate_block, up_block, down_block)
    shared_out = jnp.dot(
        shared_mask,
        normalized_rows.reshape(token_count, TILE_ROWS, -1).swapaxes(0, 1).reshape(
            TILE_ROWS * token_count, -1
        ),
        preferred_element_type=jnp.float32,
    ).astype(jnp.bfloat16)
    shared_in = across(shared_out.reshape(columns, -1, shared_out.shape[1])).reshape(-1, model_width)
    pack_rows = around(normalized_rows)
    near, far = gather_ring(shared_in)
    direct_out = jnp.einsum(
        "rq,rm->qm",
        direct_mask,
        jnp.concatenate(pack_rows, axis=0),
        preferred_element_type=jnp.float32,
    ).astype(jnp.bfloat16)
    direct_count = direct_out.shape[0]
    direct_rows = across(direct_out.reshape(columns, -1, model_width))
    block = shared_in.shape[0]
    seats = lax.axis_size("seq")
    parts = expert(
        near, near_gate, *weights, seats, ((0, 0, block), (1, block, block), (3, 2 * block, block))
    )
    parts = expert(far, far_gate, *weights, seats, ((2, 0, block),), into=parts)
    parts, direct_rows = lax.optimization_barrier((parts, direct_rows))
    direct_parts = expert(
        [direct_rows.reshape(direct_count, model_width)],
        direct_gate,
        *weights,
        1,
        ((0, 0, direct_count),),
    )
    direct_back = across(direct_parts.reshape(columns, -1, model_width))
    shared_sums = lax.psum_scatter(
        parts.reshape(-1, model_width), "seq", scatter_dimension=0, tiled=True
    )
    shared_back = across(shared_sums.reshape(columns, SHARED_SLOTS * TILE_ROWS, -1))
    pack_sums = jnp.einsum(
        "rq,qm->rm",
        direct_mask,
        direct_back.reshape(direct_count, model_width),
        preferred_element_type=jnp.float32,
    ).astype(jnp.bfloat16)
    shared_total = jnp.einsum(
        "qa,qc->ac",
        shared_mask,
        shared_back.reshape(shared_mask.shape[0], -1),
        preferred_element_type=jnp.float32,
    )
    total = hidden + shared_total.reshape(TILE_ROWS, token_count, -1).swapaxes(0, 1).reshape(
        token_count, model_width
    )
    for part in back_around(by_owner(pack_sums)):
        total = total + part.astype(jnp.float32)
    return total.astype(jnp.bfloat16)[None]


def solution(mesh):
    return jax.shard_map(
        local,
        mesh=mesh,
        in_specs=(
            P("exp", "seq", None),
            P("exp", "seq", None),
            P("exp", "seq", None),
            P("exp", "seq", None),
            P("exp", None),
            P("exp", "seq", None),
            P("exp", "seq", None),
            P("seq", "exp"),
            P(),
            P("exp", "seq", None, None),
            P("exp", "seq", None, None),
            P("exp", "seq", None, None),
        ),
        out_specs=P("exp", "seq", None),
        check_vma=False,
    )
```

```python
import functools
import math

import jax
import jax.numpy as jnp
from jax import lax
from jax.experimental import pallas as pl
from jax.experimental.pallas import tpu as pltpu
from jax.sharding import PartitionSpec as P

HEAD_DIM = 128
EXP_COL = 2


epsilon = 1e-06


def episode_ids(length_row, position_count):
    bounds = jnp.cumsum(length_row)
    position = jnp.arange(position_count, dtype=jnp.int32)
    return jnp.sum((position[:, None] >= bounds[None, :]).astype(jnp.int32), axis=1)


def attend(query_rows, key_rows, value_rows, episode):
    row_count = query_rows.shape[0]
    groups = key_rows.shape[1] // HEAD_DIM
    per_group = query_rows.shape[1] // HEAD_DIM // groups
    q_heads = query_rows.reshape(row_count, groups, per_group, HEAD_DIM)
    k_heads = key_rows.reshape(row_count, groups, HEAD_DIM)
    v_heads = value_rows.reshape(row_count, groups, HEAD_DIM)
    scores = jnp.einsum(
        "tgpd,ugd->gptu", q_heads, k_heads, preferred_element_type=jnp.float32
    ) / math.sqrt(HEAD_DIM)
    position = jnp.arange(row_count, dtype=jnp.int32)
    allowed = (episode[:, None] == episode[None, :]) & (position[None, :] <= position[:, None])
    scores = jnp.where(allowed, scores, -jnp.inf)
    row_maximum = jnp.max(scores, axis=-1, keepdims=True)
    weights = jnp.exp(scores - row_maximum)
    probability = (weights / jnp.sum(weights, axis=-1, keepdims=True)).astype(jnp.bfloat16)
    mixed = jnp.einsum("gptu,ugd->tgpd", probability, v_heads, preferred_element_type=jnp.float32)
    return mixed.astype(jnp.bfloat16).reshape(row_count, groups * per_group * HEAD_DIM)


SHARED_SLOTS = 6
TILE_ROWS = 8


CHUNK = 1024


def expert_kernel(sizes, places, aliased, *refs):
    count = len(sizes)
    pieces, (gate_ref, wg_ref, wu_ref, wd_ref) = refs[:count], refs[count : count + 4]
    out_ref, x_ref, wg_buf, wu_buf, wd_buf, g_ref, u_ref, y_ref, in_sems, out_sems = refs[
        count + 4 + aliased :
    ]
    chunks, out_chunks = x_ref.shape[0], wd_buf.shape[0]
    seats = out_ref.shape[0]
    seat = lax.axis_index("seq") if seats > 1 else 0

    def span(at):
        return pl.ds(pl.multiple_of(at * CHUNK, CHUNK), CHUNK)

    def loads(k):
        at = 0
        for i, size in enumerate(sizes):
            yield pltpu.make_async_copy(
                pieces[i].at[:, span(k)], x_ref.at[k, pl.ds(at, size)], in_sems.at[k, i]
            )
            at += size
        yield pltpu.make_async_copy(wg_ref.at[span(k)], wg_buf.at[k], in_sems.at[k, count])
        yield pltpu.make_async_copy(wu_ref.at[span(k)], wu_buf.at[k], in_sems.at[k, count + 1])

    def down_load(n):
        return pltpu.make_async_copy(
            wd_ref.at[:, span(n)], wd_buf.at[n], in_sems.at[n, count + 2]
        )

    def stores(n):
        slot = lax.rem(n, 2)
        for i, (offset, start, size) in enumerate(places):
            yield pltpu.make_async_copy(
                y_ref.at[slot, pl.ds(start, size)],
                out_ref.at[lax.rem(seat + offset, seats), :, span(n)],
                out_sems.at[slot, i],
            )

    for k in range(chunks):
        for c in loads(k):
            c.start()
    for n in range(out_chunks):
        down_load(n).start()

    g_ref[...] = jnp.zeros_like(g_ref)
    u_ref[...] = jnp.zeros_like(u_ref)

    def up(k, carry):
        for c in loads(k):
            c.wait()
        x = x_ref[k]
        g_ref[...] += jnp.dot(x, wg_buf[k], preferred_element_type=jnp.float32)
        u_ref[...] += jnp.dot(x, wu_buf[k], preferred_element_type=jnp.float32)
        return carry

    lax.fori_loop(0, chunks, up, 0)
    g = g_ref[...]
    act = (g / (1.0 + jnp.exp(-g)) * u_ref[...]).astype(jnp.bfloat16)

    def down(n, carry):
        down_load(n).wait()

        @pl.when(n >= 2)
        def _():
            for c in stores(n - 2):
                c.wait()

        y = jnp.dot(act, wd_buf[n], preferred_element_type=jnp.float32)
        y = y.astype(jnp.bfloat16).astype(jnp.float32) * gate_ref[...]
        y_ref[lax.rem(n, 2)] = y.astype(jnp.bfloat16)
        for c in stores(n):
            c.start()
        return carry

    lax.fori_loop(0, out_chunks, down, 0)
    for n in (out_chunks - 2, out_chunks - 1):
        for c in stores(n):
            c.wait()


def expert(pieces, gate, w_gate, w_up, w_down, seats, places, into=None):
    width, ff = w_gate.shape
    sizes = tuple(p.shape[0] for p in pieces)
    total = sum(sizes)
    chunks = width // CHUNK
    any_space = pl.BlockSpec(memory_space=pl.ANY)
    aliased = 0 if into is None else 1
    return pl.pallas_call(
        functools.partial(expert_kernel, sizes, places, aliased),
        in_specs=[any_space for _ in pieces]
        + [pl.BlockSpec(memory_space=pltpu.VMEM)]
        + [any_space] * (3 + aliased),
        out_specs=any_space,
        out_shape=jax.ShapeDtypeStruct((seats, places[0][2], width), jnp.bfloat16),
        scratch_shapes=[
            pltpu.VMEM((chunks, total, CHUNK), jnp.bfloat16),
            pltpu.VMEM((chunks, CHUNK, ff), jnp.bfloat16),
            pltpu.VMEM((chunks, CHUNK, ff), jnp.bfloat16),
            pltpu.VMEM((chunks, ff, CHUNK), jnp.bfloat16),
            pltpu.VMEM((total, ff), jnp.float32),
            pltpu.VMEM((total, ff), jnp.float32),
            pltpu.VMEM((2, total, CHUNK), jnp.bfloat16),
            pltpu.SemaphoreType.DMA((chunks, len(pieces) + 3)),
            pltpu.SemaphoreType.DMA((2, len(places))),
        ],
        input_output_aliases={len(pieces) + 4: 0} if aliased else {},
        compiler_params=pltpu.CompilerParams(vmem_limit_bytes=50 * 1024 * 1024),
        cost_estimate=pl.CostEstimate(
            flops=60 * total * width * ff,
            transcendentals=total * ff,
            bytes_accessed=2 * (3 * width * ff + 2 * total * width),
        ),
        name="expert",
    )(*pieces, gate, w_gate, w_up, w_down, *(() if into is None else (into,)))


def ring(rows, step):
    count = lax.axis_size("seq")
    return lax.ppermute(rows, "seq", [(i, (i + step) % count) for i in range(count)])


def around(rows):
    return [rows] + [ring(rows, -k) for k in range(1, lax.axis_size("seq"))]


def back_around(parts):
    return [parts[0]] + [ring(p, k) for k, p in enumerate(parts) if k]


def gather_ring(rows):
    half = rows.shape[0] // 2
    left, right = ring(rows, 1), ring(rows, -1)
    return [rows, right, left], [ring(left[:half], 1), ring(right[half:], -1)]


def across(blocks):
    return lax.all_to_all(blocks, "exp", split_axis=0, concat_axis=0, tiled=True)


def local(
    queries,
    key_heads,
    value_heads,
    residual,
    lengths,
    routes,
    gate_weights,
    out_weight,
    norm_gain,
    w_gate,
    w_up,
    w_down,
):
    columns = lax.axis_size("exp")
    token_count = residual.shape[1]
    model_width = residual.shape[2]

    routed = routes[0]
    node_count = routed.shape[1]
    capacity = max(2, 5 * token_count * node_count // (4 * columns))
    column = jnp.arange(columns, dtype=jnp.int32)
    slot = jnp.arange(capacity, dtype=jnp.int32)

    def slots_of(named):
        on_node = named[:, :, None] == column[None, None, :]
        member = jnp.sum(on_node.astype(jnp.int32), axis=1)
        before = jnp.cumsum(member, axis=0) - member
        return on_node, (before[:, :, None] == slot[None, None, :]) & (member[:, :, None] > 0)

    on_node, lookup = slots_of(routed)
    lookups = [slots_of(named)[1] for named in around(routed)]
    gate_pair = gate_weights[0].reshape(token_count, node_count, EXP_COL).astype(jnp.float32)
    node_route_gate = jnp.einsum(
        "tnc,tne->tce", on_node.astype(jnp.float32), gate_pair, precision=lax.Precision.HIGHEST
    )
    slot_gate = jnp.einsum(
        "qnr,qny->nyr",
        lookup.astype(jnp.float32),
        node_route_gate,
        precision=lax.Precision.HIGHEST,
    ).astype(jnp.bfloat16)
    gate_in = across(slot_gate.reshape(columns, EXP_COL * capacity))
    expert_pick = lax.axis_index("seq") // (lax.axis_size("seq") // EXP_COL)
    gates = [
        lax.dynamic_index_in_dim(
            g.reshape(columns, EXP_COL, capacity), expert_pick, axis=1, keepdims=False
        ).astype(jnp.float32)
        for g in around(gate_in)
    ]
    direct = capacity - SHARED_SLOTS
    part = jnp.arange(TILE_ROWS)
    shared_mask = (
        (
            lookup[:, :, :SHARED_SLOTS].transpose(1, 2, 0)[:, :, None, None, :]
            & (part[:, None] == part[None, :])[None, None, :, :, None]
        )
        .reshape(columns * SHARED_SLOTS * TILE_ROWS, TILE_ROWS * token_count)
        .astype(jnp.bfloat16)
    )
    ring_gates = [g[:, :SHARED_SLOTS].reshape(-1) for g in gates]
    near_gate = jnp.concatenate([ring_gates[i] for i in (0, 1, 3)])[:, None]
    far_gate = ring_gates[2][:, None]
    direct_gate = jnp.stack([g[:, SHARED_SLOTS:] for g in gates], axis=1).reshape(-1, 1)
    offset = jnp.arange(len(lookups))
    direct_masks = [
        (m[:, :, None, SHARED_SLOTS:] & (offset[None, None, :, None] == i))
        .reshape(token_count, -1)
        .astype(jnp.bfloat16)
        for i, m in enumerate(lookups)
    ]
    direct_mask = jnp.concatenate(direct_masks, axis=0)

    whole_q, whole_k, whole_v = (
        lax.all_to_all(queries[0], "seq", split_axis=1, concat_axis=0, tiled=True),
        lax.all_to_all(key_heads[0], "seq", split_axis=1, concat_axis=0, tiled=True),
        lax.all_to_all(value_heads[0], "seq", split_axis=1, concat_axis=0, tiled=True),
    )
    episode = episode_ids(lengths[0], whole_q.shape[0])
    mixed = attend(whole_q, whole_k, whole_v, episode)
    mixed, near_gate, far_gate, direct_gate, direct_mask, shared_mask = (
        lax.optimization_barrier(
            (mixed, near_gate, far_gate, direct_gate, direct_mask, shared_mask)
        )
    )
    turned = lax.dynamic_slice_in_dim(
        jnp.concatenate([mixed, mixed], axis=0),
        lax.axis_index("seq") * token_count,
        mixed.shape[0],
        axis=0,
    )
    whole_weight = lax.all_gather(out_weight, "exp", axis=1, tiled=True)

    def by_owner(rows):
        return [rows[i : i + token_count] for i in range(0, rows.shape[0], token_count)]

    sides, side = [], model_width // 2
    for at in range(0, model_width, side):
        head_partial = jnp.dot(
            turned, whole_weight[:, at : at + side], preferred_element_type=jnp.float32
        ).astype(jnp.bfloat16)
        summed = residual[0, :, at : at + side].astype(jnp.float32)
        for part in back_around(by_owner(head_partial)):
            summed = summed + part.astype(jnp.float32)
        sides.append(summed)
    hidden = jnp.concatenate(sides, axis=1)
    inverse = lax.rsqrt(jnp.mean(hidden * hidden, axis=1, keepdims=True) + epsilon)
    normalized_rows = (hidden * inverse * norm_gain[None, :]).astype(jnp.bfloat16)

    gate_block, up_block, down_block = w_gate[0, 0], w_up[0, 0], w_down[0, 0]
    weights = (gate_block, up_block, down_block)
    shared_out = jnp.dot(
        shared_mask,
        normalized_rows.reshape(token_count, TILE_ROWS, -1).swapaxes(0, 1).reshape(
            TILE_ROWS * token_count, -1
        ),
        preferred_element_type=jnp.float32,
    ).astype(jnp.bfloat16)
    shared_in = across(shared_out.reshape(columns, -1, shared_out.shape[1])).reshape(-1, model_width)
    shared_in, pack_rows = lax.optimization_barrier((shared_in, around(normalized_rows)))
    near, far = gather_ring(shared_in)
    direct_out = jnp.einsum(
        "rq,rm->qm",
        direct_mask,
        jnp.concatenate(pack_rows, axis=0),
        preferred_element_type=jnp.float32,
    ).astype(jnp.bfloat16)
    direct_count = direct_out.shape[0]
    direct_rows = across(direct_out.reshape(columns, -1, model_width))
    block = shared_in.shape[0]
    seats = lax.axis_size("seq")
    parts = expert(
        near, near_gate, *weights, seats, ((0, 0, block), (1, block, block), (3, 2 * block, block))
    )
    parts = expert(far, far_gate, *weights, seats, ((2, 0, block),), into=parts)
    parts, direct_rows = lax.optimization_barrier((parts, direct_rows))
    direct_parts = expert(
        [direct_rows.reshape(direct_count, model_width)],
        direct_gate,
        *weights,
        1,
        ((0, 0, direct_count),),
    )
    direct_back = across(direct_parts.reshape(columns, -1, model_width))
    shared_sums = lax.psum_scatter(
        parts.reshape(-1, model_width), "seq", scatter_dimension=0, tiled=True
    )
    shared_back = across(shared_sums.reshape(columns, SHARED_SLOTS * TILE_ROWS, -1))
    pack_sums = jnp.einsum(
        "rq,qm->rm",
        direct_mask,
        direct_back.reshape(direct_count, model_width),
        preferred_element_type=jnp.float32,
    ).astype(jnp.bfloat16)
    shared_total = jnp.einsum(
        "qa,qc->ac",
        shared_mask,
        shared_back.reshape(shared_mask.shape[0], -1),
        preferred_element_type=jnp.float32,
    )
    total = hidden + shared_total.reshape(TILE_ROWS, token_count, -1).swapaxes(0, 1).reshape(
        token_count, model_width
    )
    for part in back_around(by_owner(pack_sums)):
        total = total + part.astype(jnp.float32)
    return total.astype(jnp.bfloat16)[None]


def solution(mesh):
    return jax.shard_map(
        local,
        mesh=mesh,
        in_specs=(
            P("exp", "seq", None),
            P("exp", "seq", None),
            P("exp", "seq", None),
            P("exp", "seq", None),
            P("exp", None),
            P("exp", "seq", None),
            P("exp", "seq", None),
            P("seq", "exp"),
            P(),
            P("exp", "seq", None, None),
            P("exp", "seq", None, None),
            P("exp", "seq", None, None),
        ),
        out_specs=P("exp", "seq", None),
        check_vma=False,
    )
```

```python
import functools
import math

import jax
import jax.numpy as jnp
from jax import lax
from jax.experimental import pallas as pl
from jax.experimental.pallas import tpu as pltpu
from jax.sharding import PartitionSpec as P

HEAD_DIM = 128
EXP_COL = 2


epsilon = 1e-06


def episode_ids(length_row, position_count):
    bounds = jnp.cumsum(length_row)
    position = jnp.arange(position_count, dtype=jnp.int32)
    return jnp.sum((position[:, None] >= bounds[None, :]).astype(jnp.int32), axis=1)


def attend(query_rows, key_rows, value_rows, episode):
    row_count = query_rows.shape[0]
    groups = key_rows.shape[1] // HEAD_DIM
    per_group = query_rows.shape[1] // HEAD_DIM // groups
    q_heads = query_rows.reshape(row_count, groups, per_group, HEAD_DIM)
    k_heads = key_rows.reshape(row_count, groups, HEAD_DIM)
    v_heads = value_rows.reshape(row_count, groups, HEAD_DIM)
    scores = jnp.einsum(
        "tgpd,ugd->gptu", q_heads, k_heads, preferred_element_type=jnp.float32
    ) / math.sqrt(HEAD_DIM)
    position = jnp.arange(row_count, dtype=jnp.int32)
    allowed = (episode[:, None] == episode[None, :]) & (position[None, :] <= position[:, None])
    scores = jnp.where(allowed, scores, -jnp.inf)
    row_maximum = jnp.max(scores, axis=-1, keepdims=True)
    weights = jnp.exp(scores - row_maximum)
    probability = (weights / jnp.sum(weights, axis=-1, keepdims=True)).astype(jnp.bfloat16)
    mixed = jnp.einsum("gptu,ugd->tgpd", probability, v_heads, preferred_element_type=jnp.float32)
    return mixed.astype(jnp.bfloat16).reshape(row_count, groups * per_group * HEAD_DIM)


SHARED_SLOTS = 6
ROW_PIECES = 4


CHUNK = 1024


def expert_kernel(sizes, places, aliased, *refs):
    count = len(sizes)
    pieces, (gate_ref, wg_ref, wu_ref, wd_ref) = refs[:count], refs[count : count + 4]
    out_ref, x_ref, wg_buf, wu_buf, wd_buf, g_ref, u_ref, y_ref, in_sems, out_sems = refs[
        count + 4 + aliased :
    ]
    chunks, out_chunks = x_ref.shape[0], wd_buf.shape[0]
    seats = out_ref.shape[0]
    seat = lax.axis_index("seq") if seats > 1 else 0

    def span(at):
        return pl.ds(pl.multiple_of(at * CHUNK, CHUNK), CHUNK)

    def loads(k):
        at = 0
        for i, size in enumerate(sizes):
            yield pltpu.make_async_copy(
                pieces[i].at[:, span(k)], x_ref.at[k, pl.ds(at, size)], in_sems.at[k, i]
            )
            at += size
        yield pltpu.make_async_copy(wg_ref.at[span(k)], wg_buf.at[k], in_sems.at[k, count])
        yield pltpu.make_async_copy(wu_ref.at[span(k)], wu_buf.at[k], in_sems.at[k, count + 1])

    def down_load(n):
        return pltpu.make_async_copy(
            wd_ref.at[:, span(n)], wd_buf.at[n], in_sems.at[n, count + 2]
        )

    def stores(n):
        slot = lax.rem(n, 2)
        for i, (offset, start, size) in enumerate(places):
            yield pltpu.make_async_copy(
                y_ref.at[slot, pl.ds(start, size)],
                out_ref.at[lax.rem(seat + offset, seats), :, span(n)],
                out_sems.at[slot, i],
            )

    for k in range(chunks):
        for c in loads(k):
            c.start()
    for n in range(out_chunks):
        down_load(n).start()

    g_ref[...] = jnp.zeros_like(g_ref)
    u_ref[...] = jnp.zeros_like(u_ref)

    def up(k, carry):
        for c in loads(k):
            c.wait()
        x = x_ref[k]
        g_ref[...] += jnp.dot(x, wg_buf[k], preferred_element_type=jnp.float32)
        u_ref[...] += jnp.dot(x, wu_buf[k], preferred_element_type=jnp.float32)
        return carry

    lax.fori_loop(0, chunks, up, 0)
    g = g_ref[...]
    act = (g / (1.0 + jnp.exp(-g)) * u_ref[...]).astype(jnp.bfloat16)

    def down(n, carry):
        down_load(n).wait()

        @pl.when(n >= 2)
        def _():
            for c in stores(n - 2):
                c.wait()

        y = jnp.dot(act, wd_buf[n], preferred_element_type=jnp.float32)
        y = y.astype(jnp.bfloat16).astype(jnp.float32) * gate_ref[...]
        y_ref[lax.rem(n, 2)] = y.astype(jnp.bfloat16)
        for c in stores(n):
            c.start()
        return carry

    lax.fori_loop(0, out_chunks, down, 0)
    for n in (out_chunks - 2, out_chunks - 1):
        for c in stores(n):
            c.wait()


def expert(pieces, gate, w_gate, w_up, w_down, seats, places, into=None):
    width, ff = w_gate.shape
    sizes = tuple(p.shape[0] for p in pieces)
    total = sum(sizes)
    chunks = width // CHUNK
    any_space = pl.BlockSpec(memory_space=pl.ANY)
    aliased = 0 if into is None else 1
    return pl.pallas_call(
        functools.partial(expert_kernel, sizes, places, aliased),
        in_specs=[any_space for _ in pieces]
        + [pl.BlockSpec(memory_space=pltpu.VMEM)]
        + [any_space] * (3 + aliased),
        out_specs=any_space,
        out_shape=jax.ShapeDtypeStruct((seats, places[0][2], width), jnp.bfloat16),
        scratch_shapes=[
            pltpu.VMEM((chunks, total, CHUNK), jnp.bfloat16),
            pltpu.VMEM((chunks, CHUNK, ff), jnp.bfloat16),
            pltpu.VMEM((chunks, CHUNK, ff), jnp.bfloat16),
            pltpu.VMEM((chunks, ff, CHUNK), jnp.bfloat16),
            pltpu.VMEM((total, ff), jnp.float32),
            pltpu.VMEM((total, ff), jnp.float32),
            pltpu.VMEM((2, total, CHUNK), jnp.bfloat16),
            pltpu.SemaphoreType.DMA((chunks, len(pieces) + 3)),
            pltpu.SemaphoreType.DMA((2, len(places))),
        ],
        input_output_aliases={len(pieces) + 4: 0} if aliased else {},
        compiler_params=pltpu.CompilerParams(vmem_limit_bytes=50 * 1024 * 1024),
        cost_estimate=pl.CostEstimate(
            flops=60 * total * width * ff,
            transcendentals=total * ff,
            bytes_accessed=2 * (3 * width * ff + 2 * total * width),
        ),
        name="expert",
    )(*pieces, gate, w_gate, w_up, w_down, *(() if into is None else (into,)))


PROJECT_BLOCKS = 4


def project_kernel(x_ref, w_ref, *out_refs):
    depth = x_ref.shape[1]
    w = jnp.concatenate([w_ref[pl.ds(i * depth, depth)] for i in range(PROJECT_BLOCKS)], axis=1)
    y = jnp.dot(x_ref[...], w, preferred_element_type=jnp.float32).astype(jnp.bfloat16)
    size = out_refs[0].shape[0]
    for i, out in enumerate(out_refs):
        out[...] = y[i * size : (i + 1) * size]


def project(x, weight_blocks, first_column, column_count, rows_each):
    rows, depth = x.shape
    block = weight_blocks.shape[1]
    step = PROJECT_BLOCKS * block
    skip = first_column // step
    owners = rows // rows_each
    return pl.pallas_call(
        project_kernel,
        grid=(column_count // step,),
        in_specs=[
            pl.BlockSpec((rows, depth), lambda i: (0, 0)),
            pl.BlockSpec((PROJECT_BLOCKS * depth, block), lambda i: (skip + i, 0)),
        ],
        out_specs=[pl.BlockSpec((rows_each, step), lambda i: (0, i))] * owners,
        out_shape=[jax.ShapeDtypeStruct((rows_each, column_count), jnp.bfloat16)] * owners,
        compiler_params=pltpu.CompilerParams(vmem_limit_bytes=32 * 1024 * 1024),
        cost_estimate=pl.CostEstimate(
            flops=2 * rows * depth * column_count,
            transcendentals=0,
            bytes_accessed=2 * (rows * depth + depth * column_count + rows * column_count),
        ),
        name="project",
    )(x, weight_blocks)


def ring(rows, step):
    count = lax.axis_size("seq")
    return lax.ppermute(rows, "seq", [(i, (i + step) % count) for i in range(count)])


def around(rows):
    return [rows] + [ring(rows, -k) for k in range(1, lax.axis_size("seq"))]


def back_around(parts):
    return [parts[0]] + [ring(p, k) for k, p in enumerate(parts) if k]


def gather_ring(rows):
    half = rows.shape[0] // 2
    left, right = ring(rows, 1), ring(rows, -1)
    return [rows, right, left], [ring(left[:half], 1), ring(right[half:], -1)]


def across(blocks):
    return lax.all_to_all(blocks, "exp", split_axis=0, concat_axis=0, tiled=True)


def local(
    queries,
    key_heads,
    value_heads,
    residual,
    lengths,
    routes,
    gate_weights,
    out_weight,
    norm_gain,
    w_gate,
    w_up,
    w_down,
):
    columns = lax.axis_size("exp")
    token_count = residual.shape[1]
    model_width = residual.shape[2]

    routed = routes[0]
    node_count = routed.shape[1]
    capacity = max(2, 5 * token_count * node_count // (4 * columns))
    column = jnp.arange(columns, dtype=jnp.int32)
    slot = jnp.arange(capacity, dtype=jnp.int32)

    def slots_of(named):
        on_node = named[:, :, None] == column[None, None, :]
        member = jnp.sum(on_node.astype(jnp.int32), axis=1)
        before = jnp.cumsum(member, axis=0) - member
        return on_node, (before[:, :, None] == slot[None, None, :]) & (member[:, :, None] > 0)

    on_node, lookup = slots_of(routed)
    lookups = [slots_of(named)[1] for named in around(routed)]
    gate_pair = gate_weights[0].reshape(token_count, node_count, EXP_COL).astype(jnp.float32)
    node_route_gate = jnp.einsum(
        "tnc,tne->tce", on_node.astype(jnp.float32), gate_pair, precision=lax.Precision.HIGHEST
    )
    slot_gate = jnp.einsum(
        "qnr,qny->nyr",
        lookup.astype(jnp.float32),
        node_route_gate,
        precision=lax.Precision.HIGHEST,
    ).astype(jnp.bfloat16)
    gate_in = across(slot_gate.reshape(columns, EXP_COL * capacity))
    expert_pick = lax.axis_index("seq") // (lax.axis_size("seq") // EXP_COL)
    gates = [
        lax.dynamic_index_in_dim(
            g.reshape(columns, EXP_COL, capacity), expert_pick, axis=1, keepdims=False
        ).astype(jnp.float32)
        for g in around(gate_in)
    ]
    direct = capacity - SHARED_SLOTS
    part = jnp.arange(ROW_PIECES)
    shared_mask = (
        (
            lookup[:, :, :SHARED_SLOTS].transpose(1, 2, 0)[:, :, None, None, :]
            & (part[:, None] == part[None, :])[None, None, :, :, None]
        )
        .reshape(columns * SHARED_SLOTS * ROW_PIECES, ROW_PIECES * token_count)
        .astype(jnp.bfloat16)
    )
    ring_gates = [g[:, :SHARED_SLOTS].reshape(-1) for g in gates]
    near_gate = jnp.concatenate([ring_gates[i] for i in (0, 1, 3)])[:, None]
    far_gate = ring_gates[2][:, None]
    direct_gate = jnp.stack([g[:, SHARED_SLOTS:] for g in gates], axis=1).reshape(-1, 1)
    offset = jnp.arange(len(lookups))
    direct_masks = [
        (m[:, :, None, SHARED_SLOTS:] & (offset[None, None, :, None] == i))
        .reshape(token_count, -1)
        .astype(jnp.bfloat16)
        for i, m in enumerate(lookups)
    ]
    direct_mask = jnp.concatenate(direct_masks, axis=0)

    whole_q, whole_k, whole_v = (
        lax.all_to_all(queries[0], "seq", split_axis=1, concat_axis=0, tiled=True),
        lax.all_to_all(key_heads[0], "seq", split_axis=1, concat_axis=0, tiled=True),
        lax.all_to_all(value_heads[0], "seq", split_axis=1, concat_axis=0, tiled=True),
    )
    episode = episode_ids(lengths[0], whole_q.shape[0])
    mixed = attend(whole_q, whole_k, whole_v, episode)
    mixed, near_gate, far_gate, direct_gate, direct_mask, shared_mask = (
        lax.optimization_barrier(
            (mixed, near_gate, far_gate, direct_gate, direct_mask, shared_mask)
        )
    )
    turned = lax.dynamic_slice_in_dim(
        jnp.concatenate([mixed, mixed], axis=0),
        lax.axis_index("seq") * token_count,
        mixed.shape[0],
        axis=0,
    )
    whole_weight = lax.all_gather(out_weight, "exp", axis=0, tiled=True)

    def by_owner(rows):
        return [rows[i : i + token_count] for i in range(0, rows.shape[0], token_count)]

    sides, side = [], model_width // 2
    for at in range(0, model_width, side):
        summed = residual[0, :, at : at + side].astype(jnp.float32)
        for part in back_around(project(turned, whole_weight, at, side, token_count)):
            summed = summed + part.astype(jnp.float32)
        sides.append(summed)
    hidden = jnp.concatenate(sides, axis=1)
    inverse = lax.rsqrt(jnp.mean(hidden * hidden, axis=1, keepdims=True) + epsilon)
    normalized_rows = (hidden * inverse * norm_gain[None, :]).astype(jnp.bfloat16)

    gate_block, up_block, down_block = w_gate[0, 0], w_up[0, 0], w_down[0, 0]
    weights = (gate_block, up_block, down_block)
    shared_out = jnp.dot(
        shared_mask,
        normalized_rows.reshape(token_count, ROW_PIECES, -1).swapaxes(0, 1).reshape(
            ROW_PIECES * token_count, -1
        ),
        preferred_element_type=jnp.float32,
    ).astype(jnp.bfloat16)
    shared_in = across(shared_out.reshape(columns, -1, shared_out.shape[1])).reshape(-1, model_width)
    shared_in, pack_rows = lax.optimization_barrier((shared_in, around(normalized_rows)))
    near, far = gather_ring(shared_in)
    direct_out = jnp.einsum(
        "rq,rm->qm",
        direct_mask,
        jnp.concatenate(pack_rows, axis=0),
        preferred_element_type=jnp.float32,
    ).astype(jnp.bfloat16)
    direct_count = direct_out.shape[0]
    direct_rows = across(direct_out.reshape(columns, -1, model_width))
    block = shared_in.shape[0]
    seats = lax.axis_size("seq")
    parts = expert(
        near, near_gate, *weights, seats, ((0, 0, block), (1, block, block), (3, 2 * block, block))
    )
    parts = expert(far, far_gate, *weights, seats, ((2, 0, block),), into=parts)
    parts, direct_rows = lax.optimization_barrier((parts, direct_rows))
    direct_parts = expert(
        [direct_rows.reshape(direct_count, model_width)],
        direct_gate,
        *weights,
        1,
        ((0, 0, direct_count),),
    )
    direct_back = across(direct_parts.reshape(columns, -1, model_width))
    shared_sums = lax.psum_scatter(
        parts.reshape(-1, model_width), "seq", scatter_dimension=0, tiled=True
    )
    shared_back = across(shared_sums.reshape(columns, SHARED_SLOTS * ROW_PIECES, -1))
    pack_sums = jnp.einsum(
        "rq,qm->rm",
        direct_mask,
        direct_back.reshape(direct_count, model_width),
        preferred_element_type=jnp.float32,
    ).astype(jnp.bfloat16)
    shared_total = jnp.einsum(
        "qa,qc->ac",
        shared_mask,
        shared_back.reshape(shared_mask.shape[0], -1),
        preferred_element_type=jnp.float32,
    )
    total = hidden + shared_total.reshape(ROW_PIECES, token_count, -1).swapaxes(0, 1).reshape(
        token_count, model_width
    )
    for part in back_around(by_owner(pack_sums)):
        total = total + part.astype(jnp.float32)
    return total.astype(jnp.bfloat16)[None]


def solution(mesh):
    return jax.shard_map(
        local,
        mesh=mesh,
        in_specs=(
            P("exp", "seq", None),
            P("exp", "seq", None),
            P("exp", "seq", None),
            P("exp", "seq", None),
            P("exp", None),
            P("exp", "seq", None),
            P("exp", "seq", None),
            P("seq", "exp"),
            P(),
            P("exp", "seq", None, None),
            P("exp", "seq", None, None),
            P("exp", "seq", None, None),
        ),
        out_specs=P("exp", "seq", None),
        check_vma=False,
    )
```

```python
import functools
import math

import jax
import jax.numpy as jnp
from jax import lax
from jax.experimental import pallas as pl
from jax.experimental.pallas import tpu as pltpu
from jax.sharding import PartitionSpec as P

HEAD_DIM = 128
EXP_COL = 2


epsilon = 1e-06


def episode_ids(length_row, position_count):
    bounds = jnp.cumsum(length_row)
    position = jnp.arange(position_count, dtype=jnp.int32)
    return jnp.sum((position[:, None] >= bounds[None, :]).astype(jnp.int32), axis=1)


def attend(query_rows, key_rows, value_rows, episode):
    row_count = query_rows.shape[0]
    groups = key_rows.shape[1] // HEAD_DIM
    per_group = query_rows.shape[1] // HEAD_DIM // groups
    q_heads = query_rows.reshape(row_count, groups, per_group, HEAD_DIM)
    k_heads = key_rows.reshape(row_count, groups, HEAD_DIM)
    v_heads = value_rows.reshape(row_count, groups, HEAD_DIM)
    scores = jnp.einsum(
        "tgpd,ugd->gptu", q_heads, k_heads, preferred_element_type=jnp.float32
    ) / math.sqrt(HEAD_DIM)
    position = jnp.arange(row_count, dtype=jnp.int32)
    allowed = (episode[:, None] == episode[None, :]) & (position[None, :] <= position[:, None])
    scores = jnp.where(allowed, scores, -jnp.inf)
    row_maximum = jnp.max(scores, axis=-1, keepdims=True)
    weights = jnp.exp(scores - row_maximum)
    probability = (weights / jnp.sum(weights, axis=-1, keepdims=True)).astype(jnp.bfloat16)
    mixed = jnp.einsum("gptu,ugd->tgpd", probability, v_heads, preferred_element_type=jnp.float32)
    return mixed.astype(jnp.bfloat16).reshape(row_count, groups * per_group * HEAD_DIM)


SHARED_SLOTS = 6
ROW_PIECES = 4


CHUNK = 1024


def expert_kernel(sizes, places, aliased, *refs):
    count = len(sizes)
    pieces, (gate_ref, wg_ref, wu_ref, wd_ref) = refs[:count], refs[count : count + 4]
    out_ref, x_ref, wg_buf, wu_buf, wd_buf, g_ref, u_ref, y_ref, in_sems, out_sems = refs[
        count + 4 + aliased :
    ]
    chunks, out_chunks = x_ref.shape[0], wd_buf.shape[0]
    seats = out_ref.shape[0]
    seat = lax.axis_index("seq") if seats > 1 else 0

    def span(at):
        return pl.ds(pl.multiple_of(at * CHUNK, CHUNK), CHUNK)

    def loads(k):
        at = 0
        for i, size in enumerate(sizes):
            yield pltpu.make_async_copy(
                pieces[i].at[:, span(k)], x_ref.at[k, pl.ds(at, size)], in_sems.at[k, i]
            )
            at += size
        yield pltpu.make_async_copy(wg_ref.at[span(k)], wg_buf.at[k], in_sems.at[k, count])
        yield pltpu.make_async_copy(wu_ref.at[span(k)], wu_buf.at[k], in_sems.at[k, count + 1])

    def down_load(n):
        return pltpu.make_async_copy(
            wd_ref.at[:, span(n)], wd_buf.at[n], in_sems.at[n, count + 2]
        )

    def stores(n):
        slot = lax.rem(n, 2)
        for i, (offset, start, size) in enumerate(places):
            yield pltpu.make_async_copy(
                y_ref.at[slot, pl.ds(start, size)],
                out_ref.at[lax.rem(seat + offset, seats), :, span(n)],
                out_sems.at[slot, i],
            )

    for k in range(chunks):
        for c in loads(k):
            c.start()
    for n in range(out_chunks):
        down_load(n).start()

    g_ref[...] = jnp.zeros_like(g_ref)
    u_ref[...] = jnp.zeros_like(u_ref)

    def up(k, carry):
        for c in loads(k):
            c.wait()
        x = x_ref[k]
        g_ref[...] += jnp.dot(x, wg_buf[k], preferred_element_type=jnp.float32)
        u_ref[...] += jnp.dot(x, wu_buf[k], preferred_element_type=jnp.float32)
        return carry

    lax.fori_loop(0, chunks, up, 0)
    g = g_ref[...]
    act = (g / (1.0 + jnp.exp(-g)) * u_ref[...]).astype(jnp.bfloat16)

    def down(n, carry):
        down_load(n).wait()

        @pl.when(n >= 2)
        def _():
            for c in stores(n - 2):
                c.wait()

        y = jnp.dot(act, wd_buf[n], preferred_element_type=jnp.float32)
        y = y.astype(jnp.bfloat16).astype(jnp.float32) * gate_ref[...]
        y_ref[lax.rem(n, 2)] = y.astype(jnp.bfloat16)
        for c in stores(n):
            c.start()
        return carry

    lax.fori_loop(0, out_chunks, down, 0)
    for n in (out_chunks - 2, out_chunks - 1):
        for c in stores(n):
            c.wait()


def expert(pieces, gate, w_gate, w_up, w_down, seats, places, into=None):
    width, ff = w_gate.shape
    sizes = tuple(p.shape[0] for p in pieces)
    total = sum(sizes)
    chunks = width // CHUNK
    any_space = pl.BlockSpec(memory_space=pl.ANY)
    aliased = 0 if into is None else 1
    return pl.pallas_call(
        functools.partial(expert_kernel, sizes, places, aliased),
        in_specs=[any_space for _ in pieces]
        + [pl.BlockSpec(memory_space=pltpu.VMEM)]
        + [any_space] * (3 + aliased),
        out_specs=any_space,
        out_shape=jax.ShapeDtypeStruct((seats, places[0][2], width), jnp.bfloat16),
        scratch_shapes=[
            pltpu.VMEM((chunks, total, CHUNK), jnp.bfloat16),
            pltpu.VMEM((chunks, CHUNK, ff), jnp.bfloat16),
            pltpu.VMEM((chunks, CHUNK, ff), jnp.bfloat16),
            pltpu.VMEM((chunks, ff, CHUNK), jnp.bfloat16),
            pltpu.VMEM((total, ff), jnp.float32),
            pltpu.VMEM((total, ff), jnp.float32),
            pltpu.VMEM((2, total, CHUNK), jnp.bfloat16),
            pltpu.SemaphoreType.DMA((chunks, len(pieces) + 3)),
            pltpu.SemaphoreType.DMA((2, len(places))),
        ],
        input_output_aliases={len(pieces) + 4: 0} if aliased else {},
        compiler_params=pltpu.CompilerParams(vmem_limit_bytes=50 * 1024 * 1024),
        cost_estimate=pl.CostEstimate(
            flops=60 * total * width * ff,
            transcendentals=total * ff,
            bytes_accessed=2 * (3 * width * ff + 2 * total * width),
        ),
        name="expert",
    )(*pieces, gate, w_gate, w_up, w_down, *(() if into is None else (into,)))


PROJECT_BLOCKS = 4


def project_kernel(x_ref, w_ref, *out_refs):
    depth = x_ref.shape[1]
    w = jnp.concatenate([w_ref[pl.ds(i * depth, depth)] for i in range(PROJECT_BLOCKS)], axis=1)
    y = jnp.dot(x_ref[...], w, preferred_element_type=jnp.float32).astype(jnp.bfloat16)
    size = out_refs[0].shape[0]
    for i, out in enumerate(out_refs):
        out[...] = y[i * size : (i + 1) * size]


def project(x, weight_blocks, first_column, column_count, rows_each):
    rows, depth = x.shape
    block = weight_blocks.shape[1]
    step = PROJECT_BLOCKS * block
    skip = first_column // step
    owners = rows // rows_each
    return pl.pallas_call(
        project_kernel,
        grid=(column_count // step,),
        in_specs=[
            pl.BlockSpec((rows, depth), lambda i: (0, 0)),
            pl.BlockSpec((PROJECT_BLOCKS * depth, block), lambda i: (skip + i, 0)),
        ],
        out_specs=[pl.BlockSpec((rows_each, step), lambda i: (0, i))] * owners,
        out_shape=[jax.ShapeDtypeStruct((rows_each, column_count), jnp.bfloat16)] * owners,
        compiler_params=pltpu.CompilerParams(vmem_limit_bytes=32 * 1024 * 1024),
        cost_estimate=pl.CostEstimate(
            flops=2 * rows * depth * column_count,
            transcendentals=0,
            bytes_accessed=2 * (rows * depth + depth * column_count + rows * column_count),
        ),
        name="project",
    )(x, weight_blocks)


def ring(rows, step):
    count = lax.axis_size("seq")
    return lax.ppermute(rows, "seq", [(i, (i + step) % count) for i in range(count)])


def around(rows):
    return [rows] + [ring(rows, -k) for k in range(1, lax.axis_size("seq"))]


def back_around(parts):
    return [parts[0]] + [ring(p, k) for k, p in enumerate(parts) if k]


def gather_ring(rows):
    half = rows.shape[0] // 2
    left, right = ring(rows, 1), ring(rows, -1)
    return [rows, right, left], [ring(left[:half], 1), ring(right[half:], -1)]


def across(blocks):
    return lax.all_to_all(blocks, "exp", split_axis=0, concat_axis=0, tiled=True)


def local(
    queries,
    key_heads,
    value_heads,
    residual,
    lengths,
    routes,
    gate_weights,
    out_weight,
    norm_gain,
    w_gate,
    w_up,
    w_down,
):
    columns = lax.axis_size("exp")
    token_count = residual.shape[1]
    model_width = residual.shape[2]

    routed = routes[0]
    node_count = routed.shape[1]
    capacity = max(2, 5 * token_count * node_count // (4 * columns))
    column = jnp.arange(columns, dtype=jnp.int32)
    slot = jnp.arange(capacity, dtype=jnp.int32)

    def slots_of(named):
        on_node = named[:, :, None] == column[None, None, :]
        member = jnp.sum(on_node.astype(jnp.int32), axis=1)
        before = jnp.cumsum(member, axis=0) - member
        return on_node, (before[:, :, None] == slot[None, None, :]) & (member[:, :, None] > 0)

    on_node, lookup = slots_of(routed)
    lookups = [slots_of(named)[1] for named in around(routed)]
    gate_pair = gate_weights[0].reshape(token_count, node_count, EXP_COL).astype(jnp.float32)
    node_route_gate = jnp.einsum(
        "tnc,tne->tce", on_node.astype(jnp.float32), gate_pair, precision=lax.Precision.HIGHEST
    )
    slot_gate = jnp.einsum(
        "qnr,qny->nyr",
        lookup.astype(jnp.float32),
        node_route_gate,
        precision=lax.Precision.HIGHEST,
    ).astype(jnp.bfloat16)
    gate_in = across(slot_gate.reshape(columns, EXP_COL * capacity))
    expert_pick = lax.axis_index("seq") // (lax.axis_size("seq") // EXP_COL)
    gates = [
        lax.dynamic_index_in_dim(
            g.reshape(columns, EXP_COL, capacity), expert_pick, axis=1, keepdims=False
        ).astype(jnp.float32)
        for g in around(gate_in)
    ]
    direct = capacity - SHARED_SLOTS
    part = jnp.arange(ROW_PIECES)
    shared_mask = (
        (
            lookup[:, :, :SHARED_SLOTS].transpose(1, 2, 0)[:, :, None, None, :]
            & (part[:, None] == part[None, :])[None, None, :, :, None]
        )
        .reshape(columns * SHARED_SLOTS * ROW_PIECES, ROW_PIECES * token_count)
        .astype(jnp.bfloat16)
    )
    ring_gates = [g[:, :SHARED_SLOTS].reshape(-1) for g in gates]
    near_gate = jnp.concatenate([ring_gates[i] for i in (0, 1, 3)])[:, None]
    far_gate = ring_gates[2][:, None]
    direct_gate = jnp.stack([g[:, SHARED_SLOTS:] for g in gates], axis=1).reshape(-1, 1)
    offset = jnp.arange(len(lookups))
    direct_masks = [
        (m[:, :, None, SHARED_SLOTS:] & (offset[None, None, :, None] == i))
        .reshape(token_count, -1)
        .astype(jnp.bfloat16)
        for i, m in enumerate(lookups)
    ]
    direct_mask = jnp.concatenate(direct_masks, axis=0)

    whole_q, whole_k, whole_v = (
        lax.all_to_all(queries[0], "seq", split_axis=1, concat_axis=0, tiled=True),
        lax.all_to_all(key_heads[0], "seq", split_axis=1, concat_axis=0, tiled=True),
        lax.all_to_all(value_heads[0], "seq", split_axis=1, concat_axis=0, tiled=True),
    )
    episode = episode_ids(lengths[0], whole_q.shape[0])
    mixed = attend(whole_q, whole_k, whole_v, episode)
    mixed, near_gate, far_gate, direct_gate, direct_mask, shared_mask = (
        lax.optimization_barrier(
            (mixed, near_gate, far_gate, direct_gate, direct_mask, shared_mask)
        )
    )
    turned = lax.dynamic_slice_in_dim(
        jnp.concatenate([mixed, mixed], axis=0),
        lax.axis_index("seq") * token_count,
        mixed.shape[0],
        axis=0,
    )
    whole_weight = lax.all_gather(out_weight, "exp", axis=0, tiled=True)

    def by_owner(rows):
        return [rows[i : i + token_count] for i in range(0, rows.shape[0], token_count)]

    sides, side = [], model_width // 2
    for at in range(0, model_width, side):
        summed = residual[0, :, at : at + side].astype(jnp.float32)
        for part in back_around(project(turned, whole_weight, at, side, token_count)):
            summed = summed + part.astype(jnp.float32)
        sides.append(summed)
    hidden = jnp.concatenate(sides, axis=1)
    inverse = lax.rsqrt(jnp.mean(hidden * hidden, axis=1, keepdims=True) + epsilon)
    normalized_rows = (hidden * inverse * norm_gain[None, :]).astype(jnp.bfloat16)

    gate_block, up_block, down_block = w_gate[0, 0], w_up[0, 0], w_down[0, 0]
    weights = (gate_block, up_block, down_block)
    shared_out = jnp.dot(
        shared_mask,
        normalized_rows.reshape(token_count, ROW_PIECES, -1).swapaxes(0, 1).reshape(
            ROW_PIECES * token_count, -1
        ),
        preferred_element_type=jnp.float32,
    ).astype(jnp.bfloat16)
    shared_in = across(shared_out.reshape(columns, -1, shared_out.shape[1])).reshape(-1, model_width)
    shared_in, pack_rows = lax.optimization_barrier((shared_in, around(normalized_rows)))
    near, far = gather_ring(shared_in)
    direct_out = jnp.einsum(
        "rq,rm->qm",
        direct_mask,
        jnp.concatenate(pack_rows, axis=0),
        preferred_element_type=jnp.float32,
    ).astype(jnp.bfloat16)
    direct_count = direct_out.shape[0]
    direct_rows = across(direct_out.reshape(columns, -1, model_width))
    block = shared_in.shape[0]
    seats = lax.axis_size("seq")
    parts = expert(
        near, near_gate, *weights, seats, ((0, 0, block), (1, block, block), (3, 2 * block, block))
    )
    parts = expert(far, far_gate, *weights, seats, ((2, 0, block),), into=parts)
    parts, direct_rows = lax.optimization_barrier((parts, direct_rows))
    direct_parts = expert(
        [direct_rows.reshape(direct_count, model_width)],
        direct_gate,
        *weights,
        1,
        ((0, 0, direct_count),),
    )
    direct_back = across(direct_parts.reshape(columns, -1, model_width))
    shared_sums = lax.psum_scatter(
        parts.reshape(-1, model_width), "seq", scatter_dimension=0, tiled=True
    )
    shared_back = across(shared_sums.reshape(columns, SHARED_SLOTS * ROW_PIECES, -1))
    back_rows = direct_back.reshape(direct_count, model_width)
    pack_sums = [
        jnp.einsum("rq,qm->rm", mask, back_rows, preferred_element_type=jnp.float32).astype(
            jnp.bfloat16
        )
        for mask in by_owner(direct_mask)
    ]
    shared_total = jnp.einsum(
        "qa,qc->ac",
        shared_mask,
        shared_back.reshape(shared_mask.shape[0], -1),
        preferred_element_type=jnp.float32,
    )
    total = hidden + shared_total.reshape(ROW_PIECES, token_count, -1).swapaxes(0, 1).reshape(
        token_count, model_width
    )
    for part in back_around(pack_sums):
        total = total + part.astype(jnp.float32)
    return total.astype(jnp.bfloat16)[None]


def solution(mesh):
    return jax.shard_map(
        local,
        mesh=mesh,
        in_specs=(
            P("exp", "seq", None),
            P("exp", "seq", None),
            P("exp", "seq", None),
            P("exp", "seq", None),
            P("exp", None),
            P("exp", "seq", None),
            P("exp", "seq", None),
            P("seq", "exp"),
            P(),
            P("exp", "seq", None, None),
            P("exp", "seq", None, None),
            P("exp", "seq", None, None),
        ),
        out_specs=P("exp", "seq", None),
        check_vma=False,
    )
```
